32 devices in a mesh: groups: 2 (over y), gx: 4 (over z), gy: 2 (over x), col: 2 (over core).
Axes of the slice: x: 2, y: 2, z: 4, core: 2. Of those that a mesh axis runs over, the one named last changes fastest.
Arguments:
- volume: bfloat16 [32, 16, 2048], P(('groups', 'gx'), ('gy', 'col')), parts along dimension 0, may hold values from -6 to 6
- fine_kernel: bfloat16 [27, 64, 64], replicated, may hold values from -0.15625 to 0.15625
- fine_bias: float32 [64], replicated, may hold values from -3 to 3
- down_kernel: bfloat16 [512, 512], replicated, may hold values from -0.25 to 0.25
- down_bias: float32 [512], replicated, may hold values from -3 to 3
- bottle_kernel: bfloat16 [27, 512, 1024], P(None, None, 'gx'), may hold values from -0.0546875 to 0.0546875
- bottle_bias: float32 [1024], P('gx'), may hold values from -3 to 3
- up_kernel: bfloat16 [1024, 512], replicated, may hold values from -0.1875 to 0.1875
- up_bias: float32 [64], replicated, may hold values from -3 to 3
Outputs:
- decoded: bfloat16 [32, 16, 2048], P(('groups', 'gx'), ('gy', 'col')), parts along dimension 0
The draws below stay inside these ranges and needn't reach their ends.
There are 2 independent parts, one for each index of `groups`. The reference program is written for one: setup_inputs(seed, part) draws one part's arguments, and reference() takes and returns one part's arrays. A program takes and returns all parts, laid end to end along the dimension named above; an argument that names none is the same for every part. Nothing has to cross between parts.
All inputs are finite; a program needn't handle non-finite values.
Results may differ from the reference program's by a relative error of at most 0.0047.
Values may be sent and summed in bfloat16 or wider, within the bound.
A program may use at most 128 MiB of HBM per device.

```python
import jax
import jax.numpy as jnp

C = 64
CD = 512
CB = 1024
NZ = 32
NX = 16
NY = 16


def levels(key, shape, pieces, least, largest):
    factor_of = 1.0
    for position, parts in pieces:
        steps = jax.random.uniform(jax.random.fold_in(jax.random.fold_in(key, 6), position), (parts,), jnp.float32, least / len(pieces), largest / len(pieces))
        factor_of = factor_of * jnp.repeat(jnp.exp(steps), shape[position] // parts).reshape((-1,) + (1,) * (len(shape) - 1 - position))
    return factor_of


def normal_values(key, dims, deviation, limit, cuts=(), kind=jnp.bfloat16):
    result = deviation * jax.random.normal(key, dims, jnp.float32)
    if cuts:
        result = result * levels(key, dims, cuts, -0.22, 0.18)
    return jnp.clip(result, -limit, limit).astype(kind)


def setup_inputs(seed: int = 0, part: int = 0) -> dict:
    splits = jax.random.split(jax.random.key(seed), 10)
    part_splits = jax.random.split(jax.random.fold_in(splits[9], part), 10)
    volume = normal_values(part_splits[0], (NX, NY, NZ * C), 1.0, 6.0, ((0, 4), (1, 4)))
    fine_kernel = normal_values(splits[1], (27, C, C), (27 * C) ** -0.5, 0.15625)
    fine_bias = normal_values(splits[2], (C,), 0.5, 3.0, (), jnp.float32)
    down_kernel = normal_values(splits[3], (8 * C, CD), (8 * C) ** -0.5, 0.25)
    down_bias = normal_values(splits[4], (CD,), 0.5, 3.0, (), jnp.float32)
    bottle_kernel = normal_values(splits[5], (27, CD, CB), (27 * CD) ** -0.5, 0.0546875, ((2, 4),))
    bottle_bias = normal_values(splits[6], (CB,), 0.5, 3.0, ((0, 4),), jnp.float32)
    up_kernel = normal_values(splits[7], (CB, 8 * C), CB ** -0.5, 0.1875)
    up_bias = normal_values(splits[8], (C,), 0.5, 3.0, (), jnp.float32)
    return dict(volume=volume, fine_kernel=fine_kernel, fine_bias=fine_bias, down_kernel=down_kernel, down_bias=down_bias, bottle_kernel=bottle_kernel, bottle_bias=bottle_bias, up_kernel=up_kernel, up_bias=up_bias)


def conv_three(padded, kernel, bias, nx, ny, nz):
    chans = padded.shape[3]
    total = jnp.zeros((nx * ny * nz, kernel.shape[2]), jnp.float32)
    for i in range(3):
        for j in range(3):
            for k in range(3):
                piece = padded[i:i + nx, j:j + ny, k:k + nz, :].reshape(nx * ny * nz, chans)
                total = total + jnp.dot(piece, kernel[i * 9 + j * 3 + k], preferred_element_type=jnp.float32)
    return (total + bias[None, :]).reshape(nx, ny, nz, kernel.shape[2])


def reference(volume, fine_kernel, fine_bias, down_kernel, down_bias, bottle_kernel, bottle_bias, up_kernel, up_bias):
    cells = volume.reshape(NX, NY, NZ, C)
    padded = jnp.pad(cells, ((1, 1), (1, 1), (1, 1), (0, 0)))
    fine = jax.nn.silu(conv_three(padded, fine_kernel, fine_bias, NX, NY, NZ)).astype(jnp.bfloat16)
    hx, hy, hz = NX // 2, NY // 2, NZ // 2
    blocks = fine.reshape(hx, 2, hy, 2, hz, 2, C).transpose(0, 2, 4, 1, 3, 5, 6).reshape(hx * hy * hz, 8 * C)
    coarse = jax.nn.silu(jnp.dot(blocks, down_kernel, preferred_element_type=jnp.float32) + down_bias[None, :]).astype(jnp.bfloat16)
    coarse = coarse.reshape(hx, hy, hz, CD)
    cpad = jnp.pad(coarse, ((1, 1), (1, 1), (1, 1), (0, 0)))
    bottle = jax.nn.silu(conv_three(cpad, bottle_kernel, bottle_bias, hx, hy, hz)).astype(jnp.bfloat16)
    lifted = jnp.dot(bottle.reshape(hx * hy * hz, CB), up_kernel, preferred_element_type=jnp.float32)
    lifted = lifted.reshape(hx, hy, hz, 8, C) + up_bias[None, None, None, None, :]
    lifted = lifted.reshape(hx, hy, hz, 2, 2, 2, C).transpose(0, 3, 1, 4, 2, 5, 6).reshape(NX, NY, NZ, C)
    decoded = (fine.astype(jnp.float32) + lifted).astype(jnp.bfloat16)
    return decoded.reshape(NX, NY, NZ * C)
```

```python
import functools

import jax
import jax.numpy as jnp
from jax import lax
from jax.experimental import pallas as pl
from jax.experimental.pallas import tpu as pltpu
from jax.sharding import PartitionSpec as P

MESH = pl.DeviceIdType.MESH
F32 = jnp.float32
BF16 = jnp.bfloat16


def silu(a):
    return (0.5 * a) * (1.0 + jnp.tanh(0.5 * a))


def shifted(a, amount, depth):
    rows = a.shape[0]
    z = lax.broadcasted_iota(jnp.int32, a.shape, 0) % depth
    moved = pltpu.roll(a, amount % rows, 0)
    keep = z >= amount if amount > 0 else z < depth + amount
    return jnp.where(keep, moved, 0.0)


def body(
    sizes,
    vol_hbm,
    fk_hbm,
    fb_ref,
    dk_hbm,
    db_ref,
    bk_hbm,
    bb_ref,
    uk_hbm,
    ub_ref,
    out_ref,
    brick,
    fk,
    band,
    dk,
    bk,
    uk,
    fine_ref,
    strip,
    acc,
    sent,
    back,
    load_sem,
    halo_send,
    halo_recv,
    gather_send,
    gather_recv,
    swap_send,
    swap_recv,
):
    ngx, ngy, ncol = sizes
    nq = ngy * ncol
    cx, cy = out_ref.shape[0], out_ref.shape[1]
    depth, pair = out_ref.shape[2], out_ref.shape[3]
    chans = pair // 2
    hx, hy = cx // 2, cy // 2
    cd = dk.shape[1]
    cb = bk.shape[2]
    g = lax.axis_index("gx")
    q = lax.axis_index("gy") * ncol + lax.axis_index("col")

    def device(gg, qq):
        return {"gx": gg, "gy": qq // ncol, "col": qq % ncol}

    loads = [
        pltpu.make_async_copy(src, dst, load_sem.at[n])
        for n, (src, dst) in enumerate(
            (
                (vol_hbm, brick.at[pl.ds(1, cx), pl.ds(1, cy)]),
                (fk_hbm, fk),
                (dk_hbm, dk),
                (bk_hbm, bk),
                (uk_hbm, uk),
            )
        )
    ]
    for load in loads:
        load.start()

    brick[0] = jnp.zeros_like(brick[0])
    brick[cx + 1] = jnp.zeros_like(brick[0])
    for y in (0, cy + 1):
        brick[1 : cx + 1, y] = jnp.zeros((cx, depth, pair), BF16)
    strip[0] = jnp.zeros_like(strip[0])
    strip[ngx * hx + 1] = jnp.zeros_like(strip[0])

    @pl.when(q == 0)
    def _():
        strip[1 : ngx * hx + 1, 0] = jnp.zeros((ngx * hx, depth, cd), BF16)

    @pl.when(q == nq - 1)
    def _():
        strip[1 : ngx * hx + 1, hy + 1] = jnp.zeros((ngx * hx, depth, cd), BF16)

    barrier = pltpu.get_barrier_semaphore()
    for b in (-1, 0, 1):
        there = jnp.logical_and(q + b >= 0, q + b < nq)

        @pl.when(there)
        def _():
            for d in range(ngx):
                if d or b:
                    pl.semaphore_signal(
                        barrier,
                        inc=1,
                        device_id=device(lax.rem(g + d, ngx), q + b),
                        device_id_type=MESH,
                    )

    inner = jnp.logical_and(q > 0, q < nq - 1)
    pl.semaphore_wait(barrier, jnp.where(inner, 3 * ngx - 1, 2 * ngx - 1))
    loads[0].wait()

    def remote(src, dst, send, recv, gg, qq):
        return pltpu.make_async_remote_copy(
            src_ref=src,
            dst_ref=dst,
            send_sem=send,
            recv_sem=recv,
            device_id=device(gg, qq),
            device_id_type=MESH,
        )

    def edges(step, count):
        if step == 0:
            return pl.ds(1, count), pl.ds(1, count)
        if step > 0:
            return pl.ds(count, 1), pl.ds(0, 1)
        return pl.ds(1, 1), pl.ds(count + 1, 1)

    def valid(gg, qq):
        ok = jnp.logical_and(gg >= 0, gg < ngx)
        return jnp.logical_and(ok, jnp.logical_and(qq >= 0, qq < nq))

    halos = []
    for a in (-1, 0, 1):
        for b in (-1, 0, 1):
            if a == 0 and b == 0:
                continue
            t = len(halos)
            sx, dx = edges(a, cx)
            sy, dy = edges(b, cy)
            halos.append(
                (
                    valid(g + a, q + b),
                    remote(
                        brick.at[sx, sy], brick.at[dx, dy],
                        halo_send.at[t], halo_recv.at[t], g + a, q + b,
                    ),
                    valid(g - a, q - b),
                    remote(
                        brick.at[dx, dy], brick.at[dx, dy],
                        halo_send.at[t], halo_recv.at[t], g - a, q - b,
                    ),
                )
            )
    for ok, out, _, _ in halos:
        pl.when(ok)(out.start)

    loads[1].wait()
    empty = jnp.zeros((chans, chans), BF16)
    for ij in range(9):
        f0, f1, f2 = fk[3 * ij], fk[3 * ij + 1], fk[3 * ij + 2]
        band[ij * pair : ij * pair + chans] = jnp.concatenate([f1, f0, empty, f2], axis=1)
        band[ij * pair + chans : (ij + 1) * pair] = jnp.concatenate([f2, f1, f0, empty], axis=1)

    for _, _, ok, into in halos:
        pl.when(ok)(into.wait_recv)

    pieces = [
        brick[i : i + cx, j : j + cy].reshape(cx * cy * depth, pair)
        for i in range(3)
        for j in range(3)
    ]
    prod = jnp.dot(jnp.concatenate(pieces, axis=1), band[...], preferred_element_type=F32)
    side = prod[:, pair:]
    lane = lax.broadcasted_iota(jnp.int32, side.shape, 1)
    fb = fb_ref[...]
    total = (
        prod[:, :pair]
        + jnp.where(lane < chans, shifted(side, 1, depth), shifted(side, -1, depth))
        + jnp.concatenate([fb, fb], axis=1)
    )
    fine_ref[...] = silu(total).astype(BF16).reshape(cx, cy, depth, pair)

    loads[2].wait()
    cells = []
    for x in range(hx):
        for y in range(hy):
            cells.append(
                jnp.concatenate(
                    [fine_ref[2 * x + dx, 2 * y + dy] for dx in (0, 1) for dy in (0, 1)], axis=1
                )
            )
    coarse = jnp.dot(jnp.concatenate(cells, axis=0), dk[...], preferred_element_type=F32)
    coarse = silu(coarse + db_ref[...]).astype(BF16)
    strip[pl.ds(1 + hx * g, hx), 1 : hy + 1] = coarse.reshape(hx, hy, depth, cd)

    gathers = []
    for d in range(ngx - 1, -1, -1):
        to, source = lax.rem(g + d, ngx), lax.rem(g - d + ngx, ngx)
        for b in (0, -1, 1):
            if d == 0 and b == 0:
                continue
            sy, dy = edges(b, hy)
            s = gather_send.at[d, b + 1]
            r = gather_recv.at[d, b + 1]
            mine, theirs = pl.ds(1 + hx * g, hx), pl.ds(1 + hx * source, hx)
            gathers.append(
                (
                    valid(g, q + b),
                    remote(strip.at[mine, sy], strip.at[mine, dy], s, r, to, q + b),
                    valid(g, q - b),
                    remote(strip.at[theirs, dy], strip.at[theirs, dy], s, r, source, q - b),
                )
            )
    for ok, out, _, _ in gathers:
        pl.when(ok)(out.start)
    loads[3].wait()
    loads[4].wait()
    for _, _, ok, into in gathers:
        pl.when(ok)(into.wait_recv)

    rows = ngx * hx * hy * depth
    acc[...] = jnp.zeros_like(acc)

    @pl.loop(0, 9)
    def _(ij):
        i, j = ij // 3, ij % 3
        lhs = strip[pl.ds(i, ngx * hx), pl.ds(j, hy)].reshape(rows, cd)
        for k in range(3):
            acc[k] += jnp.dot(lhs, bk[3 * ij + k], preferred_element_type=F32)

    bottle = acc[1] + shifted(acc[0], 1, depth) + shifted(acc[2], -1, depth)
    bottle = silu(bottle + bb_ref[...]).astype(BF16)
    sent[...] = bottle.reshape(ngx, hx * hy * depth, cb)
    back[g] = sent[g]

    swaps = []
    for d in range(ngx - 1, 0, -1):
        to, source = lax.rem(g + d, ngx), lax.rem(g - d + ngx, ngx)
        swaps.append(
            (
                remote(sent.at[to], back.at[g], swap_send.at[d], swap_recv.at[d], to, q),
                remote(sent.at[to], back.at[source], swap_send.at[d], swap_recv.at[d], source, q),
            )
        )
    for out, _ in swaps:
        out.start()
    for _, into in swaps:
        into.wait_recv()

    lifted = jnp.zeros((hx * hy * depth, uk.shape[1]), F32)
    for p in range(ngx):
        lifted += jnp.dot(back[p], uk[p * cb : (p + 1) * cb], preferred_element_type=F32)
    ub = ub_ref[...]
    ub = jnp.concatenate([ub, ub], axis=1)
    for x in range(hx):
        for y in range(hy):
            at = (x * hy + y) * depth
            for dx in (0, 1):
                for dy in (0, 1):
                    c = (2 * dx + dy) * pair
                    out_ref[2 * x + dx, 2 * y + dy] = (
                        fine_ref[2 * x + dx, 2 * y + dy].astype(F32)
                        + (lifted[at : at + depth, c : c + pair] + ub)
                    ).astype(BF16)

    for ok, out, _, _ in halos:
        pl.when(ok)(out.wait_send)
    for ok, out, _, _ in gathers:
        pl.when(ok)(out.wait_send)
    for out, _ in swaps:
        out.wait_send()


def local(
    sizes,
    volume,
    fine_kernel,
    fine_bias,
    down_kernel,
    down_bias,
    bottle_kernel,
    bottle_bias,
    up_kernel,
    up_bias,
):
    ngx = sizes[0]
    cx, cy, merged = volume.shape
    chans = fine_kernel.shape[1]
    pair = 2 * chans
    depth = merged // pair
    hx, hy = cx // 2, cy // 2
    cd = down_kernel.shape[1]
    cb = bottle_kernel.shape[2]
    cells = hx * hy * depth
    hbm = pl.BlockSpec(memory_space=pl.ANY)
    vmem = pl.BlockSpec(memory_space=pltpu.VMEM)
    dma = pltpu.SemaphoreType.DMA
    out = pl.pallas_call(
        functools.partial(body, sizes),
        out_shape=jax.ShapeDtypeStruct((cx, cy, depth, pair), BF16),
        in_specs=[hbm, hbm, vmem, hbm, vmem, hbm, vmem, hbm, vmem],
        out_specs=vmem,
        scratch_shapes=[
            pltpu.VMEM((cx + 2, cy + 2, depth, pair), BF16),
            pltpu.VMEM(fine_kernel.shape, BF16),
            pltpu.VMEM((9 * pair, 2 * pair), BF16),
            pltpu.VMEM(down_kernel.shape, BF16),
            pltpu.VMEM(bottle_kernel.shape, BF16),
            pltpu.VMEM(up_kernel.shape, BF16),
            pltpu.VMEM((cx, cy, depth, pair), BF16),
            pltpu.VMEM((ngx * hx + 2, hy + 2, depth, cd), BF16),
            pltpu.VMEM((3, ngx * cells, cb), F32),
            pltpu.VMEM((ngx, cells, cb), BF16),
            pltpu.VMEM((ngx, cells, cb), BF16),
            dma((5,)),
            dma((8,)),
            dma((8,)),
            dma((ngx, 3)),
            dma((ngx, 3)),
            dma((ngx,)),
            dma((ngx,)),
        ],
        compiler_params=pltpu.CompilerParams(
            collective_id=0, has_side_effects=True, vmem_limit_bytes=48 << 20
        ),
    )(
        volume.reshape(cx, cy, depth, pair),
        fine_kernel,
        fine_bias.reshape(1, -1),
        down_kernel,
        down_bias.reshape(1, -1),
        bottle_kernel,
        bottle_bias.reshape(1, -1),
        up_kernel,
        up_bias.reshape(1, -1),
    )
    return out.reshape(cx, cy, merged)


def solution(mesh):
    placed = (
        P(("groups", "gx"), ("gy", "col"), None),
        P(),
        P(),
        P(),
        P(),
        P(None, None, "gx"),
        P("gx"),
        P(),
        P(),
    )
    sizes = tuple(mesh.shape[name] for name in ("gx", "gy", "col"))
    return jax.shard_map(
        functools.partial(local, sizes),
        mesh=mesh,
        in_specs=placed,
        out_specs=P(("groups", "gx"), ("gy", "col"), None),
        check_vma=False,
    )
```

```python
import functools

import jax
import jax.numpy as jnp
from jax import lax
from jax.experimental import pallas as pl
from jax.experimental.pallas import tpu as pltpu
from jax.sharding import PartitionSpec as P

MESH = pl.DeviceIdType.MESH
F32 = jnp.float32
BF16 = jnp.bfloat16


def silu(a):
    return (0.5 * a) * (1.0 + jnp.tanh(0.5 * a))


def shifted(a, amount, depth):
    rows = a.shape[0]
    z = lax.broadcasted_iota(jnp.int32, a.shape, 0) % depth
    moved = pltpu.roll(a, amount % rows, 0)
    keep = z >= amount if amount > 0 else z < depth + amount
    return jnp.where(keep, moved, 0.0)


def body(
    sizes,
    vol_hbm,
    fk_hbm,
    fb_hbm,
    dk_hbm,
    db_hbm,
    bk_hbm,
    bb_hbm,
    uk_hbm,
    ub_hbm,
    out_ref,
    brick,
    fk,
    band,
    dk,
    bk,
    uk,
    fb_ref,
    db_ref,
    bb_ref,
    ub_ref,
    fine_ref,
    strip,
    acc,
    sent,
    back,
    load_sem,
    halo_send,
    halo_recv,
    gather_send,
    gather_recv,
    swap_send,
    swap_recv,
):
    ngx, ngy, ncol = sizes
    nq = ngy * ncol
    cx, cy = out_ref.shape[0], out_ref.shape[1]
    depth, pair = out_ref.shape[2], out_ref.shape[3]
    chans = pair // 2
    hx, hy = cx // 2, cy // 2
    cd = dk.shape[1]
    cb = bk.shape[2]
    g = lax.axis_index("gx")
    q = lax.axis_index("gy") * ncol + lax.axis_index("col")

    def device(gg, qq):
        return {"gx": gg, "gy": qq // ncol, "col": qq % ncol}

    loads = [
        pltpu.make_async_copy(src, dst, load_sem.at[n])
        for n, (src, dst) in enumerate(
            (
                (vol_hbm, brick.at[pl.ds(1, cx), pl.ds(1, cy)]),
                (fk_hbm, fk),
                (fb_hbm, fb_ref),
                (dk_hbm, dk),
                (db_hbm, db_ref),
                (bb_hbm, bb_ref),
                (uk_hbm, uk),
                (ub_hbm, ub_ref),
            )
            + tuple((bk_hbm.at[pl.ds(3 * n, 3)], bk.at[pl.ds(3 * n, 3)]) for n in range(9))
        )
    ]
    for load in loads:
        load.start()

    brick[0] = jnp.zeros_like(brick[0])
    brick[cx + 1] = jnp.zeros_like(brick[0])
    for y in (0, cy + 1):
        brick[1 : cx + 1, y] = jnp.zeros((cx, depth, pair), BF16)
    strip[0] = jnp.zeros_like(strip[0])
    strip[ngx * hx + 1] = jnp.zeros_like(strip[0])

    @pl.when(q == 0)
    def _():
        strip[1 : ngx * hx + 1, 0] = jnp.zeros((ngx * hx, depth, cd), BF16)

    @pl.when(q == nq - 1)
    def _():
        strip[1 : ngx * hx + 1, hy + 1] = jnp.zeros((ngx * hx, depth, cd), BF16)

    barrier = pltpu.get_barrier_semaphore()
    for b in (-1, 0, 1):
        there = jnp.logical_and(q + b >= 0, q + b < nq)

        @pl.when(there)
        def _():
            for d in range(ngx):
                if d or b:
                    pl.semaphore_signal(
                        barrier,
                        inc=1,
                        device_id=device(lax.rem(g + d, ngx), q + b),
                        device_id_type=MESH,
                    )

    inner = jnp.logical_and(q > 0, q < nq - 1)
    pl.semaphore_wait(barrier, jnp.where(inner, 3 * ngx - 1, 2 * ngx - 1))
    loads[0].wait()

    def remote(src, dst, send, recv, gg, qq):
        return pltpu.make_async_remote_copy(
            src_ref=src,
            dst_ref=dst,
            send_sem=send,
            recv_sem=recv,
            device_id=device(gg, qq),
            device_id_type=MESH,
        )

    def edges(step, count):
        if step == 0:
            return pl.ds(1, count), pl.ds(1, count)
        if step > 0:
            return pl.ds(count, 1), pl.ds(0, 1)
        return pl.ds(1, 1), pl.ds(count + 1, 1)

    def valid(gg, qq):
        ok = jnp.logical_and(gg >= 0, gg < ngx)
        return jnp.logical_and(ok, jnp.logical_and(qq >= 0, qq < nq))

    halos = []
    for a in (-1, 0, 1):
        for b in (-1, 0, 1):
            if a == 0 and b == 0:
                continue
            t = len(halos)
            sx, dx = edges(a, cx)
            sy, dy = edges(b, cy)
            halos.append(
                (
                    valid(g + a, q + b),
                    remote(
                        brick.at[sx, sy], brick.at[dx, dy],
                        halo_send.at[t], halo_recv.at[t], g + a, q + b,
                    ),
                    valid(g - a, q - b),
                    remote(
                        brick.at[dx, dy], brick.at[dx, dy],
                        halo_send.at[t], halo_recv.at[t], g - a, q - b,
                    ),
                )
            )
    for ok, out, _, _ in halos:
        pl.when(ok)(out.start)

    loads[1].wait()
    empty = jnp.zeros((chans, chans), BF16)
    for ij in range(9):
        f0, f1, f2 = fk[3 * ij], fk[3 * ij + 1], fk[3 * ij + 2]
        band[ij * pair : ij * pair + chans] = jnp.concatenate([f1, f0, empty, f2], axis=1)
        band[ij * pair + chans : (ij + 1) * pair] = jnp.concatenate([f2, f1, f0, empty], axis=1)

    for _, _, ok, into in halos:
        pl.when(ok)(into.wait_recv)

    pieces = [
        brick[i : i + cx, j : j + cy].reshape(cx * cy * depth, pair)
        for i in range(3)
        for j in range(3)
    ]
    loads[2].wait()
    prod = jnp.dot(jnp.concatenate(pieces, axis=1), band[...], preferred_element_type=F32)
    side = prod[:, pair:]
    lane = lax.broadcasted_iota(jnp.int32, side.shape, 1)
    fb = fb_ref[...]
    total = (
        prod[:, :pair]
        + jnp.where(lane < chans, shifted(side, 1, depth), shifted(side, -1, depth))
        + jnp.concatenate([fb, fb], axis=1)
    )
    fine_ref[...] = silu(total).astype(BF16).reshape(cx, cy, depth, pair)

    loads[3].wait()
    loads[4].wait()
    cells = []
    for x in range(hx):
        for y in range(hy):
            cells.append(
                jnp.concatenate(
                    [fine_ref[2 * x + dx, 2 * y + dy] for dx in (0, 1) for dy in (0, 1)], axis=1
                )
            )
    coarse = jnp.dot(jnp.concatenate(cells, axis=0), dk[...], preferred_element_type=F32)
    coarse = silu(coarse + db_ref[...]).astype(BF16)
    strip[pl.ds(1 + hx * g, hx), 1 : hy + 1] = coarse.reshape(hx, hy, depth, cd)

    gathers = []
    for d in range(ngx - 1, -1, -1):
        to, source = lax.rem(g + d, ngx), lax.rem(g - d + ngx, ngx)
        for b in (0, -1, 1):
            if d == 0 and b == 0:
                continue
            sy, dy = edges(b, hy)
            s = gather_send.at[d, b + 1]
            r = gather_recv.at[d, b + 1]
            mine, theirs = pl.ds(1 + hx * g, hx), pl.ds(1 + hx * source, hx)
            gathers.append(
                (
                    valid(g, q + b),
                    remote(strip.at[mine, sy], strip.at[mine, dy], s, r, to, q + b),
                    valid(g, q - b),
                    remote(strip.at[theirs, dy], strip.at[theirs, dy], s, r, source, q - b),
                )
            )
    for ok, out, _, _ in gathers:
        pl.when(ok)(out.start)
    for load in loads[5:]:
        load.wait()
    for _, _, ok, into in gathers:
        pl.when(ok)(into.wait_recv)

    rows = ngx * hx * hy * depth
    acc[...] = jnp.zeros_like(acc)

    @pl.loop(0, 9)
    def _(ij):
        i, j = ij // 3, ij % 3
        lhs = strip[pl.ds(i, ngx * hx), pl.ds(j, hy)].reshape(rows, cd)
        for k in range(3):
            acc[k] += jnp.dot(lhs, bk[3 * ij + k], preferred_element_type=F32)

    bottle = acc[1] + shifted(acc[0], 1, depth) + shifted(acc[2], -1, depth)
    bottle = silu(bottle + bb_ref[...]).astype(BF16)
    sent[...] = bottle.reshape(ngx, hx * hy * depth, cb)
    back[g] = sent[g]

    swaps = []
    for d in range(ngx - 1, 0, -1):
        to, source = lax.rem(g + d, ngx), lax.rem(g - d + ngx, ngx)
        swaps.append(
            (
                remote(sent.at[to], back.at[g], swap_send.at[d], swap_recv.at[d], to, q),
                remote(sent.at[to], back.at[source], swap_send.at[d], swap_recv.at[d], source, q),
            )
        )
    for out, _ in swaps:
        out.start()
    for _, into in swaps:
        into.wait_recv()

    lifted = jnp.zeros((hx * hy * depth, uk.shape[1]), F32)
    for p in range(ngx):
        lifted += jnp.dot(back[p], uk[p * cb : (p + 1) * cb], preferred_element_type=F32)
    ub = ub_ref[...]
    ub = jnp.concatenate([ub, ub], axis=1)
    for x in range(hx):
        for y in range(hy):
            at = (x * hy + y) * depth
            for dx in (0, 1):
                for dy in (0, 1):
                    c = (2 * dx + dy) * pair
                    out_ref[2 * x + dx, 2 * y + dy] = (
                        fine_ref[2 * x + dx, 2 * y + dy].astype(F32)
                        + (lifted[at : at + depth, c : c + pair] + ub)
                    ).astype(BF16)

    for ok, out, _, _ in halos:
        pl.when(ok)(out.wait_send)
    for ok, out, _, _ in gathers:
        pl.when(ok)(out.wait_send)
    for out, _ in swaps:
        out.wait_send()


def local(
    sizes,
    volume,
    fine_kernel,
    fine_bias,
    down_kernel,
    down_bias,
    bottle_kernel,
    bottle_bias,
    up_kernel,
    up_bias,
):
    ngx = sizes[0]
    cx, cy, merged = volume.shape
    chans = fine_kernel.shape[1]
    pair = 2 * chans
    depth = merged // pair
    hx, hy = cx // 2, cy // 2
    cd = down_kernel.shape[1]
    cb = bottle_kernel.shape[2]
    cells = hx * hy * depth
    hbm = pl.BlockSpec(memory_space=pltpu.HBM)
    vmem = pl.BlockSpec(memory_space=pltpu.VMEM)
    dma = pltpu.SemaphoreType.DMA
    out = pl.pallas_call(
        functools.partial(body, sizes),
        out_shape=jax.ShapeDtypeStruct((cx, cy, depth, pair), BF16),
        in_specs=[hbm] * 9,
        out_specs=vmem,
        scratch_shapes=[
            pltpu.VMEM((cx + 2, cy + 2, depth, pair), BF16),
            pltpu.VMEM(fine_kernel.shape, BF16),
            pltpu.VMEM((9 * pair, 2 * pair), BF16),
            pltpu.VMEM(down_kernel.shape, BF16),
            pltpu.VMEM(bottle_kernel.shape, BF16),
            pltpu.VMEM(up_kernel.shape, BF16),
            pltpu.VMEM((1, chans), F32),
            pltpu.VMEM((1, cd), F32),
            pltpu.VMEM((1, cb), F32),
            pltpu.VMEM((1, chans), F32),
            pltpu.VMEM((cx, cy, depth, pair), BF16),
            pltpu.VMEM((ngx * hx + 2, hy + 2, depth, cd), BF16),
            pltpu.VMEM((3, ngx * cells, cb), F32),
            pltpu.VMEM((ngx, cells, cb), BF16),
            pltpu.VMEM((ngx, cells, cb), BF16),
            dma((17,)),
            dma((8,)),
            dma((8,)),
            dma((ngx, 3)),
            dma((ngx, 3)),
            dma((ngx,)),
            dma((ngx,)),
        ],
        compiler_params=pltpu.CompilerParams(
            collective_id=0, has_side_effects=True, vmem_limit_bytes=60 << 20
        ),
    )(
        volume.reshape(cx, cy, depth, pair),
        fine_kernel,
        fine_bias.reshape(1, -1),
        down_kernel,
        down_bias.reshape(1, -1),
        bottle_kernel,
        bottle_bias.reshape(1, -1),
        up_kernel,
        up_bias.reshape(1, -1),
    )
    return out.reshape(cx, cy, merged)


def solution(mesh):
    placed = (
        P(("groups", "gx"), ("gy", "col"), None),
        P(),
        P(),
        P(),
        P(),
        P(None, None, "gx"),
        P("gx"),
        P(),
        P(),
    )
    sizes = tuple(mesh.shape[name] for name in ("gx", "gy", "col"))
    return jax.shard_map(
        functools.partial(local, sizes),
        mesh=mesh,
        in_specs=placed,
        out_specs=P(("groups", "gx"), ("gy", "col"), None),
        check_vma=False,
    )
```

```python
import functools

import jax
import jax.numpy as jnp
from jax import lax
from jax.experimental import pallas as pl
from jax.experimental.pallas import tpu as pltpu
from jax.sharding import PartitionSpec as P

MESH = pl.DeviceIdType.MESH
F32 = jnp.float32
BF16 = jnp.bfloat16


def silu(a):
    return (0.5 * a) * (1.0 + jnp.tanh(0.5 * a))


def shifted(a, amount, depth):
    rows = a.shape[0]
    z = lax.broadcasted_iota(jnp.int32, a.shape, 0) % depth
    moved = pltpu.roll(a, amount % rows, 0)
    keep = z >= amount if amount > 0 else z < depth + amount
    return jnp.where(keep, moved, 0.0)


def body(
    sizes,
    vol_hbm,
    fk_hbm,
    fb_hbm,
    dk_hbm,
    db_hbm,
    bk_hbm,
    bb_hbm,
    uk_hbm,
    ub_hbm,
    out_ref,
    raw,
    brick,
    fk,
    band,
    dk,
    bk,
    uk,
    fb_ref,
    db_ref,
    bb_ref,
    ub_ref,
    fine_ref,
    strip,
    acc,
    sent,
    back,
    load_sem,
    halo_send,
    halo_recv,
    gather_send,
    gather_recv,
    rim_send,
    rim_recv,
    swap_send,
    swap_recv,
):
    ngx, ngy, ncol = sizes
    nq = ngy * ncol
    cx, cy = out_ref.shape[0], out_ref.shape[1]
    depth, pair = out_ref.shape[2], out_ref.shape[3]
    chans = pair // 2
    hx, hy = cx // 2, cy // 2
    cd = dk.shape[1]
    cb = bk.shape[2]
    g = lax.axis_index("gx")
    q = lax.axis_index("gy") * ncol + lax.axis_index("col")

    def device(gg, qq):
        return {"gx": gg, "gy": qq // ncol, "col": qq % ncol}

    loads = [
        pltpu.make_async_copy(src, dst, load_sem.at[n])
        for n, (src, dst) in enumerate(
            (
                (vol_hbm, raw),
                (fk_hbm, fk),
                (fb_hbm, fb_ref),
                (dk_hbm, dk),
                (db_hbm, db_ref),
                (bb_hbm, bb_ref),
                (uk_hbm, uk),
                (ub_hbm, ub_ref),
            )
            + tuple((bk_hbm.at[pl.ds(3 * n, 3)], bk.at[pl.ds(3 * n, 3)]) for n in range(9))
        )
    ]
    for load in loads:
        load.start()

    brick[0] = jnp.zeros_like(brick[0])
    brick[cx + 1] = jnp.zeros_like(brick[0])
    for y in (0, cy + 1):
        brick[1 : cx + 1, y] = jnp.zeros((cx, depth, pair), BF16)
    strip[0] = jnp.zeros_like(strip[0])
    strip[ngx * hx + 1] = jnp.zeros_like(strip[0])

    @pl.when(q == 0)
    def _():
        strip[1 : ngx * hx + 1, 0] = jnp.zeros((ngx * hx, depth, cd), BF16)

    @pl.when(q == nq - 1)
    def _():
        strip[1 : ngx * hx + 1, hy + 1] = jnp.zeros((ngx * hx, depth, cd), BF16)

    def valid(gg, qq):
        ok = jnp.logical_and(gg >= 0, gg < ngx)
        return jnp.logical_and(ok, jnp.logical_and(qq >= 0, qq < nq))

    barrier = pltpu.get_barrier_semaphore()

    def greet(gg, qq):
        pl.semaphore_signal(barrier, inc=1, device_id=device(gg, qq), device_id_type=MESH)

    partners = ngx - 1
    for b in (-1, 1):
        for a in (-1, 0, 1):
            there = valid(g + a, q + b)
            pl.when(there)(functools.partial(greet, g + a, q + b))
            partners += there.astype(jnp.int32)
    for d in range(1, ngx):
        greet(lax.rem(g + d, ngx), q)

    loads[0].wait()
    for x in range(cx):
        brick[1 + x, 1 : cy + 1] = (
            raw[x].astype(F32).reshape(cy, depth, pair).astype(BF16)
        )
    pl.semaphore_wait(barrier, partners)

    def remote(src, dst, send, recv, gg, qq):
        return pltpu.make_async_remote_copy(
            src_ref=src,
            dst_ref=dst,
            send_sem=send,
            recv_sem=recv,
            device_id=device(gg, qq),
            device_id_type=MESH,
        )

    def edges(step, count):
        if step == 0:
            return pl.ds(1, count), pl.ds(1, count)
        if step > 0:
            return pl.ds(count, 1), pl.ds(0, 1)
        return pl.ds(1, 1), pl.ds(count + 1, 1)

    halos = []
    for a in (-1, 0, 1):
        for b in (-1, 0, 1):
            if a == 0 and b == 0:
                continue
            t = len(halos)
            sx, dx = edges(a, cx)
            sy, dy = edges(b, cy)
            halos.append(
                (
                    valid(g + a, q + b),
                    remote(
                        brick.at[sx, sy], brick.at[dx, dy],
                        halo_send.at[t], halo_recv.at[t], g + a, q + b,
                    ),
                    valid(g - a, q - b),
                    remote(
                        brick.at[dx, dy], brick.at[dx, dy],
                        halo_send.at[t], halo_recv.at[t], g - a, q - b,
                    ),
                )
            )
    for ok, out, _, _ in halos:
        pl.when(ok)(out.start)

    loads[1].wait()
    empty = jnp.zeros((chans, chans), BF16)
    for ij in range(9):
        f0, f1, f2 = fk[3 * ij], fk[3 * ij + 1], fk[3 * ij + 2]
        band[ij * pair : ij * pair + chans] = jnp.concatenate([f1, f0, empty, f2], axis=1)
        band[ij * pair + chans : (ij + 1) * pair] = jnp.concatenate([f2, f1, f0, empty], axis=1)

    for _, _, ok, into in halos:
        pl.when(ok)(into.wait_recv)

    pieces = [
        brick[i : i + cx, j : j + cy].reshape(cx * cy * depth, pair)
        for i in range(3)
        for j in range(3)
    ]
    loads[2].wait()
    prod = jnp.dot(jnp.concatenate(pieces, axis=1), band[...], preferred_element_type=F32)
    side = prod[:, pair:]
    lane = lax.broadcasted_iota(jnp.int32, side.shape, 1)
    fb = fb_ref[...]
    total = (
        prod[:, :pair]
        + jnp.where(lane < chans, shifted(side, 1, depth), shifted(side, -1, depth))
        + jnp.concatenate([fb, fb], axis=1)
    )
    fine_ref[...] = silu(total).astype(BF16).reshape(cx, cy, depth, pair)

    loads[3].wait()
    loads[4].wait()
    cells = []
    for x in range(hx):
        for y in range(hy):
            cells.append(
                jnp.concatenate(
                    [fine_ref[2 * x + dx, 2 * y + dy] for dx in (0, 1) for dy in (0, 1)], axis=1
                )
            )
    coarse = jnp.dot(jnp.concatenate(cells, axis=0), dk[...], preferred_element_type=F32)
    coarse = silu(coarse + db_ref[...]).astype(BF16)
    strip[pl.ds(1 + hx * g, hx), 1 : hy + 1] = coarse.reshape(hx, hy, depth, cd)

    def planes(at):
        return pl.ds(1 + hx * at, hx)

    def block(source, to):
        ref = strip.at[planes(source), pl.ds(1, hy)]
        return remote(ref, ref, gather_send.at[to], gather_recv.at[source], to, q)

    def rim(at, b, sending):
        sy, dy = edges(b, hy)
        dst = strip.at[planes(at), dy]
        src = strip.at[planes(at), sy] if sending else dst
        t = (b + 1) // 2
        beside = q + b if sending else q - b
        return remote(src, dst, rim_send.at[at, t], rim_recv.at[at, t], g, beside)

    def rims(at, sending, action):
        for b in (-1, 1):
            other = q + b if sending else q - b
            pl.when(valid(g, other))(getattr(rim(at, b, sending), action))

    def others(visit):
        for d in range(1, ngx):
            for p in (g + d, g - d):
                pl.when(valid(p, q))(functools.partial(visit, p))

    others(lambda p: block(g, p).start())
    rims(g, True, "start")
    acc[...] = jnp.zeros_like(acc)
    for load in loads[5:]:
        load.wait()

    def part(source, columns):
        lhs = [strip[planes(source), j : j + hy].reshape(hx * hy * depth, cd) for j in columns]
        for i in range(3):
            at = pl.ds(2 + hx * source - i, hx)
            for k in range(3):
                term = sum(
                    jnp.dot(piece, bk[9 * i + 3 * j + k], preferred_element_type=F32)
                    for piece, j in zip(lhs, columns)
                )
                acc[k, at] += term.reshape(hx, hy * depth, cb)

    def source_of(n):
        return g + jnp.where(n % 2 == 1, (n + 1) // 2, -((n + 1) // 2))

    @pl.loop(0, 2 * ngx)
    def _(n):
        now, before = source_of(n), source_of(n - 1)
        ready = jnp.logical_and(valid(now, q), n < 2 * ngx - 1)

        @pl.when(jnp.logical_and(ready, n > 0))
        def _():
            block(now, now).wait_recv()
            rims(now, True, "start")

        @pl.when(jnp.logical_and(valid(before, q), n > 0))
        def _():
            rims(before, False, "wait_recv")
            part(before, (0, 2))

        @pl.when(ready)
        def _():
            part(now, (1,))

    def swap(to, source):
        return remote(sent.at[to], back.at[source], swap_send.at[to], swap_recv.at[source], to, q)

    def finish(p):
        at = pl.ds(1 + hx * p, hx)
        taps = [acc[k, at].reshape(hx * hy * depth, cb) for k in range(3)]
        bottle = taps[1] + shifted(taps[0], 1, depth) + shifted(taps[2], -1, depth)
        return silu(bottle + bb_ref[...]).astype(BF16)

    for d in range(ngx - 1, 0, -1):
        to = lax.rem(g + d, ngx)
        sent[to] = finish(to)
        swap(to, g).start()

    lifted = jnp.dot(finish(g), uk[g], preferred_element_type=F32)
    for d in range(1, ngx):
        source = lax.rem(g + d, ngx)
        swap(source, source).wait_recv()
        lifted += jnp.dot(back[source], uk[source], preferred_element_type=F32)
    ub = ub_ref[...]
    ub = jnp.concatenate([ub, ub], axis=1)
    for x in range(hx):
        for y in range(hy):
            at = (x * hy + y) * depth
            for dx in (0, 1):
                for dy in (0, 1):
                    c = (2 * dx + dy) * pair
                    out_ref[2 * x + dx, 2 * y + dy] = (
                        fine_ref[2 * x + dx, 2 * y + dy].astype(F32)
                        + (lifted[at : at + depth, c : c + pair] + ub)
                    ).astype(BF16)

    for ok, out, _, _ in halos:
        pl.when(ok)(out.wait_send)
    others(lambda p: block(g, p).wait_send())
    others(lambda p: swap(p, g).wait_send())
    for at in range(ngx):
        rims(at, True, "wait_send")


def local(
    sizes,
    volume,
    fine_kernel,
    fine_bias,
    down_kernel,
    down_bias,
    bottle_kernel,
    bottle_bias,
    up_kernel,
    up_bias,
):
    ngx = sizes[0]
    cx, cy, merged = volume.shape
    chans = fine_kernel.shape[1]
    pair = 2 * chans
    depth = merged // pair
    hx, hy = cx // 2, cy // 2
    cd = down_kernel.shape[1]
    cb = bottle_kernel.shape[2]
    cells = hx * hy * depth
    hbm = pl.BlockSpec(memory_space=pltpu.HBM)
    vmem = pl.BlockSpec(memory_space=pltpu.VMEM)
    dma = pltpu.SemaphoreType.DMA
    out = pl.pallas_call(
        functools.partial(body, sizes),
        out_shape=jax.ShapeDtypeStruct((cx, cy, depth, pair), BF16),
        in_specs=[hbm] * 9,
        out_specs=vmem,
        scratch_shapes=[
            pltpu.VMEM(volume.shape, BF16),
            pltpu.VMEM((cx + 2, cy + 2, depth, pair), BF16),
            pltpu.VMEM(fine_kernel.shape, BF16),
            pltpu.VMEM((9 * pair, 2 * pair), BF16),
            pltpu.VMEM(down_kernel.shape, BF16),
            pltpu.VMEM(bottle_kernel.shape, BF16),
            pltpu.VMEM((ngx, cb, up_kernel.shape[1]), BF16),
            pltpu.VMEM((1, chans), F32),
            pltpu.VMEM((1, cd), F32),
            pltpu.VMEM((1, cb), F32),
            pltpu.VMEM((1, chans), F32),
            pltpu.VMEM((cx, cy, depth, pair), BF16),
            pltpu.VMEM((ngx * hx + 2, hy + 2, depth, cd), BF16),
            pltpu.VMEM((3, ngx * hx + 2, hy * depth, cb), F32),
            pltpu.VMEM((ngx, cells, cb), BF16),
            pltpu.VMEM((ngx, cells, cb), BF16),
            dma((17,)),
            dma((8,)),
            dma((8,)),
            dma((ngx,)),
            dma((ngx,)),
            dma((ngx, 2)),
            dma((ngx, 2)),
            dma((ngx,)),
            dma((ngx,)),
        ],
        compiler_params=pltpu.CompilerParams(
            collective_id=0, has_side_effects=True, vmem_limit_bytes=60 << 20
        ),
    )(
        volume,
        fine_kernel,
        fine_bias.reshape(1, -1),
        down_kernel,
        down_bias.reshape(1, -1),
        bottle_kernel,
        bottle_bias.reshape(1, -1),
        up_kernel.reshape(ngx, cb, -1),
        up_bias.reshape(1, -1),
    )
    return out.reshape(cx, cy, merged)


def solution(mesh):
    placed = (
        P(("groups", "gx"), ("gy", "col"), None),
        P(),
        P(),
        P(),
        P(),
        P(None, None, "gx"),
        P("gx"),
        P(),
        P(),
    )
    sizes = tuple(mesh.shape[name] for name in ("gx", "gy", "col"))
    return jax.shard_map(
        functools.partial(local, sizes),
        mesh=mesh,
        in_specs=placed,
        out_specs=P(("groups", "gx"), ("gy", "col"), None),
        check_vma=False,
    )
```

```python
import functools

import jax
import jax.numpy as jnp
from jax import lax
from jax.experimental import pallas as pl
from jax.experimental.pallas import tpu as pltpu
from jax.sharding import PartitionSpec as P

MESH = pl.DeviceIdType.MESH
F32 = jnp.float32
BF16 = jnp.bfloat16


def silu(a):
    return (0.5 * a) * (1.0 + jnp.tanh(0.5 * a))


def shifted(a, amount, depth):
    rows = a.shape[0]
    z = lax.broadcasted_iota(jnp.int32, a.shape, 0) % depth
    moved = pltpu.roll(a, amount % rows, 0)
    keep = z >= amount if amount > 0 else z < depth + amount
    return jnp.where(keep, moved, 0.0)


def body(
    sizes,
    vol_hbm,
    fk_hbm,
    fb_hbm,
    dk_hbm,
    db_hbm,
    bk_hbm,
    bb_hbm,
    uk_hbm,
    ub_hbm,
    out_ref,
    raw,
    brick,
    fk,
    band,
    dk,
    bk,
    uk,
    fb_ref,
    db_ref,
    bb_ref,
    ub_ref,
    fine_ref,
    strip,
    acc,
    sent,
    back,
    load_sem,
    halo_send,
    halo_recv,
    gather_send,
    gather_recv,
    rim_send,
    rim_recv,
    swap_send,
    swap_recv,
):
    ngx, ngy, ncol = sizes
    nq = ngy * ncol
    cx, cy, depth, pair = fine_ref.shape
    chans = pair // 2
    hx, hy = cx // 2, cy // 2
    cd = dk.shape[1]
    cb = bk.shape[2]
    g = lax.axis_index("gx")
    q = lax.axis_index("gy") * ncol + lax.axis_index("col")

    def device(gg, qq):
        return {"gx": gg, "gy": qq // ncol, "col": qq % ncol}

    loads = [
        pltpu.make_async_copy(src, dst, load_sem.at[n])
        for n, (src, dst) in enumerate(
            (
                (vol_hbm, raw),
                (fk_hbm, fk),
                (fb_hbm, fb_ref),
                (dk_hbm, dk),
                (db_hbm, db_ref),
                (bb_hbm, bb_ref),
                (uk_hbm, uk),
                (ub_hbm, ub_ref),
            )
            + tuple((bk_hbm.at[pl.ds(3 * n, 3)], bk.at[pl.ds(3 * n, 3)]) for n in range(9))
        )
    ]
    for load in loads:
        load.start()

    brick[0] = jnp.zeros_like(brick[0])
    brick[cx + 1] = jnp.zeros_like(brick[0])
    for y in (0, cy + 1):
        brick[1 : cx + 1, y] = jnp.zeros((cx, depth, pair), BF16)
    strip[0] = jnp.zeros_like(strip[0])
    strip[ngx * hx + 1] = jnp.zeros_like(strip[0])

    @pl.when(q == 0)
    def _():
        strip[1 : ngx * hx + 1, 0] = jnp.zeros((ngx * hx, depth, cd), BF16)

    @pl.when(q == nq - 1)
    def _():
        strip[1 : ngx * hx + 1, hy + 1] = jnp.zeros((ngx * hx, depth, cd), BF16)

    def valid(gg, qq):
        ok = jnp.logical_and(gg >= 0, gg < ngx)
        return jnp.logical_and(ok, jnp.logical_and(qq >= 0, qq < nq))

    barrier = pltpu.get_barrier_semaphore()

    def greet(gg, qq):
        pl.semaphore_signal(barrier, inc=1, device_id=device(gg, qq), device_id_type=MESH)

    partners = ngx - 1
    for b in (-1, 1):
        for a in (-1, 0, 1):
            there = valid(g + a, q + b)
            pl.when(there)(functools.partial(greet, g + a, q + b))
            partners += there.astype(jnp.int32)
    for d in range(1, ngx):
        greet(lax.rem(g + d, ngx), q)

    loads[0].wait()
    for x in range(cx):
        brick[1 + x, 1 : cy + 1] = (
            raw[x].astype(F32).reshape(cy, depth, pair).astype(BF16)
        )
    pl.semaphore_wait(barrier, partners)

    def remote(src, dst, send, recv, gg, qq):
        return pltpu.make_async_remote_copy(
            src_ref=src,
            dst_ref=dst,
            send_sem=send,
            recv_sem=recv,
            device_id=device(gg, qq),
            device_id_type=MESH,
        )

    def edges(step, count):
        if step == 0:
            return pl.ds(1, count), pl.ds(1, count)
        if step > 0:
            return pl.ds(count, 1), pl.ds(0, 1)
        return pl.ds(1, 1), pl.ds(count + 1, 1)

    halos = []
    for a in (-1, 0, 1):
        for b in (-1, 0, 1):
            if a == 0 and b == 0:
                continue
            t = len(halos)
            sx, dx = edges(a, cx)
            sy, dy = edges(b, cy)
            halos.append(
                (
                    valid(g + a, q + b),
                    remote(
                        brick.at[sx, sy], brick.at[dx, dy],
                        halo_send.at[t], halo_recv.at[t], g + a, q + b,
                    ),
                    valid(g - a, q - b),
                    remote(
                        brick.at[dx, dy], brick.at[dx, dy],
                        halo_send.at[t], halo_recv.at[t], g - a, q - b,
                    ),
                )
            )
    for ok, out, _, _ in halos:
        pl.when(ok)(out.start)

    loads[1].wait()
    empty = jnp.zeros((chans, chans), BF16)
    for ij in range(9):
        f0, f1, f2 = fk[3 * ij], fk[3 * ij + 1], fk[3 * ij + 2]
        band[ij * pair : ij * pair + chans] = jnp.concatenate([f1, f0, empty, f2], axis=1)
        band[ij * pair + chans : (ij + 1) * pair] = jnp.concatenate([f2, f1, f0, empty], axis=1)

    for _, _, ok, into in halos:
        pl.when(ok)(into.wait_recv)

    pieces = [
        brick[i : i + cx, j : j + cy].reshape(cx * cy * depth, pair)
        for i in range(3)
        for j in range(3)
    ]
    loads[2].wait()
    prod = jnp.dot(jnp.concatenate(pieces, axis=1), band[...], preferred_element_type=F32)
    side = prod[:, pair:]
    lane = lax.broadcasted_iota(jnp.int32, side.shape, 1)
    fb = fb_ref[...]
    total = (
        prod[:, :pair]
        + jnp.where(lane < chans, shifted(side, 1, depth), shifted(side, -1, depth))
        + jnp.concatenate([fb, fb], axis=1)
    )
    fine_ref[...] = silu(total).astype(BF16).reshape(cx, cy, depth, pair)

    loads[3].wait()
    loads[4].wait()
    cells = []
    for x in range(hx):
        for y in range(hy):
            cells.append(
                jnp.concatenate(
                    [fine_ref[2 * x + dx, 2 * y + dy] for dx in (0, 1) for dy in (0, 1)], axis=1
                )
            )
    coarse = jnp.dot(jnp.concatenate(cells, axis=0), dk[...], preferred_element_type=F32)
    coarse = silu(coarse + db_ref[...]).astype(BF16)
    strip[pl.ds(1 + hx * g, hx), 1 : hy + 1] = coarse.reshape(hx, hy, depth, cd)

    def planes(at):
        return pl.ds(1 + hx * at, hx)

    def block(source, to):
        ref = strip.at[planes(source), pl.ds(1, hy)]
        return remote(ref, ref, gather_send.at[to], gather_recv.at[source], to, q)

    def rim(at, b, sending):
        sy, dy = edges(b, hy)
        dst = strip.at[planes(at), dy]
        src = strip.at[planes(at), sy] if sending else dst
        t = (b + 1) // 2
        beside = q + b if sending else q - b
        return remote(src, dst, rim_send.at[at, t], rim_recv.at[at, t], g, beside)

    def rims(at, sending, action):
        for b in (-1, 1):
            other = q + b if sending else q - b
            pl.when(valid(g, other))(getattr(rim(at, b, sending), action))

    def others(visit):
        for d in range(1, ngx):
            for p in (g + d, g - d):
                pl.when(valid(p, q))(functools.partial(visit, p))

    others(lambda p: block(g, p).start())
    rims(g, True, "start")
    acc[...] = jnp.zeros_like(acc)
    for load in loads[5:]:
        load.wait()

    def part(source, columns):
        lhs = [strip[planes(source), j : j + hy].reshape(hx * hy * depth, cd) for j in columns]
        for i in range(3):
            at = pl.ds(2 + hx * source - i, hx)
            for k in range(3):
                term = sum(
                    jnp.dot(piece, bk[9 * i + 3 * j + k], preferred_element_type=F32)
                    for piece, j in zip(lhs, columns)
                )
                acc[k, at] += term.reshape(hx, hy * depth, cb)

    def source_of(n):
        return g + jnp.where(n % 2 == 1, (n + 1) // 2, -((n + 1) // 2))

    def swap(to, source):
        return remote(sent.at[to], back.at[source], swap_send.at[to], swap_recv.at[source], to, q)

    def finish(p):
        at = pl.ds(1 + hx * p, hx)
        taps = [acc[k, at].reshape(hx * hy * depth, cb) for k in range(3)]
        bottle = taps[1] + shifted(taps[0], 1, depth) + shifted(taps[2], -1, depth)
        return silu(bottle + bb_ref[...]).astype(BF16)

    def position(source):
        ahead = source - g
        return jnp.where(ahead > 0, 2 * ahead - 1, -2 * ahead)

    def last_step(p):
        far = position(p)
        for beside in (p - 1, p + 1):
            far = jnp.maximum(far, jnp.where(valid(beside, q), position(beside), 0))
        return far + 1

    @pl.loop(0, 2 * ngx)
    def _(n):
        now, before = source_of(n), source_of(n - 1)
        ready = jnp.logical_and(valid(now, q), n < 2 * ngx - 1)

        @pl.when(jnp.logical_and(ready, n > 0))
        def _():
            block(now, now).wait_recv()
            rims(now, True, "start")

        @pl.when(jnp.logical_and(valid(before, q), n > 0))
        def _():
            rims(before, False, "wait_recv")
            part(before, (0, 2))

        @pl.when(ready)
        def _():
            part(now, (1,))

        @pl.loop(0, ngx)
        def _(p):
            @pl.when(jnp.logical_and(p != g, last_step(p) == n))
            def _():
                sent[p] = finish(p)
                swap(p, g).start()

    lifted = jnp.dot(finish(g), uk[g], preferred_element_type=F32)
    for d in range(1, ngx):
        source = lax.rem(g + d, ngx)
        swap(source, source).wait_recv()
        lifted += jnp.dot(back[source], uk[source], preferred_element_type=F32)
    ub = ub_ref[...]
    ub = jnp.concatenate([ub, ub], axis=1)
    for x in range(hx):
        for dx in (0, 1):
            columns = []
            for y in range(hy):
                at = (x * hy + y) * depth
                for dy in (0, 1):
                    c = (2 * dx + dy) * pair
                    columns.append(
                        fine_ref[2 * x + dx, 2 * y + dy].astype(F32)
                        + (lifted[at : at + depth, c : c + pair] + ub)
                    )
            whole = jnp.stack(columns).reshape(cy, depth * pair)
            out_ref[2 * x + dx] = whole.astype(BF16)

    for ok, out, _, _ in halos:
        pl.when(ok)(out.wait_send)
    others(lambda p: block(g, p).wait_send())
    others(lambda p: swap(p, g).wait_send())
    for at in range(ngx):
        rims(at, True, "wait_send")


def local(
    sizes,
    volume,
    fine_kernel,
    fine_bias,
    down_kernel,
    down_bias,
    bottle_kernel,
    bottle_bias,
    up_kernel,
    up_bias,
):
    ngx = sizes[0]
    cx, cy, merged = volume.shape
    chans = fine_kernel.shape[1]
    pair = 2 * chans
    depth = merged // pair
    hx, hy = cx // 2, cy // 2
    cd = down_kernel.shape[1]
    cb = bottle_kernel.shape[2]
    cells = hx * hy * depth
    hbm = pl.BlockSpec(memory_space=pltpu.HBM)
    vmem = pl.BlockSpec(memory_space=pltpu.VMEM)
    dma = pltpu.SemaphoreType.DMA
    return pl.pallas_call(
        functools.partial(body, sizes),
        out_shape=jax.ShapeDtypeStruct((cx, cy, merged), BF16),
        in_specs=[hbm] * 9,
        out_specs=vmem,
        scratch_shapes=[
            pltpu.VMEM(volume.shape, BF16),
            pltpu.VMEM((cx + 2, cy + 2, depth, pair), BF16),
            pltpu.VMEM(fine_kernel.shape, BF16),
            pltpu.VMEM((9 * pair, 2 * pair), BF16),
            pltpu.VMEM(down_kernel.shape, BF16),
            pltpu.VMEM(bottle_kernel.shape, BF16),
            pltpu.VMEM((ngx, cb, up_kernel.shape[1]), BF16),
            pltpu.VMEM((1, chans), F32),
            pltpu.VMEM((1, cd), F32),
            pltpu.VMEM((1, cb), F32),
            pltpu.VMEM((1, chans), F32),
            pltpu.VMEM((cx, cy, depth, pair), BF16),
            pltpu.VMEM((ngx * hx + 2, hy + 2, depth, cd), BF16),
            pltpu.VMEM((3, ngx * hx + 2, hy * depth, cb), F32),
            pltpu.VMEM((ngx, cells, cb), BF16),
            pltpu.VMEM((ngx, cells, cb), BF16),
            dma((17,)),
            dma((8,)),
            dma((8,)),
            dma((ngx,)),
            dma((ngx,)),
            dma((ngx, 2)),
            dma((ngx, 2)),
            dma((ngx,)),
            dma((ngx,)),
        ],
        compiler_params=pltpu.CompilerParams(
            collective_id=0, has_side_effects=True, vmem_limit_bytes=60 << 20
        ),
    )(
        volume,
        fine_kernel,
        fine_bias.reshape(1, -1),
        down_kernel,
        down_bias.reshape(1, -1),
        bottle_kernel,
        bottle_bias.reshape(1, -1),
        up_kernel.reshape(ngx, cb, -1),
        up_bias.reshape(1, -1),
    )


def solution(mesh):
    placed = (
        P(("groups", "gx"), ("gy", "col"), None),
        P(),
        P(),
        P(),
        P(),
        P(None, None, "gx"),
        P("gx"),
        P(),
        P(),
    )
    sizes = tuple(mesh.shape[name] for name in ("gx", "gy", "col"))
    return jax.shard_map(
        functools.partial(local, sizes),
        mesh=mesh,
        in_specs=placed,
        out_specs=P(("groups", "gx"), ("gy", "col"), None),
        check_vma=False,
    )
```

```python
import functools

import jax
import jax.numpy as jnp
from jax import lax
from jax.experimental import pallas as pl
from jax.experimental.pallas import tpu as pltpu
from jax.sharding import PartitionSpec as P

MESH = pl.DeviceIdType.MESH
F32 = jnp.float32
BF16 = jnp.bfloat16


def silu(a):
    return (0.5 * a) * (1.0 + jnp.tanh(0.5 * a))


def shifted(a, amount, depth):
    rows = a.shape[0]
    z = lax.broadcasted_iota(jnp.int32, a.shape, 0) % depth
    moved = pltpu.roll(a, amount % rows, 0)
    keep = z >= amount if amount > 0 else z < depth + amount
    return jnp.where(keep, moved, 0.0)


def body(
    sizes,
    vol_hbm,
    fk_hbm,
    fb_hbm,
    dk_hbm,
    db_hbm,
    bk_hbm,
    bb_hbm,
    uk_hbm,
    ub_hbm,
    out_ref,
    raw,
    brick,
    fk,
    band,
    dk,
    bk,
    uk,
    fb_ref,
    db_ref,
    bb_ref,
    ub_ref,
    fine_ref,
    strip,
    acc,
    sent,
    back,
    load_sem,
    halo_send,
    halo_recv,
    gather_send,
    gather_recv,
    rim_send,
    rim_recv,
    swap_send,
    swap_recv,
):
    ngx, ngy, ncol = sizes
    nq = ngy * ncol
    cx, cy, depth, pair = fine_ref.shape
    chans = pair // 2
    hx, hy = cx // 2, cy // 2
    cd = dk.shape[1]
    cb = bk.shape[2]
    g = lax.axis_index("gx")
    q = lax.axis_index("gy") * ncol + lax.axis_index("col")

    def device(gg, qq):
        return {"gx": gg, "gy": qq // ncol, "col": qq % ncol}

    loads = [
        pltpu.make_async_copy(src, dst, load_sem.at[n])
        for n, (src, dst) in enumerate(
            (
                (vol_hbm, raw),
                (fk_hbm, fk),
                (fb_hbm, fb_ref),
                (dk_hbm, dk),
                (db_hbm, db_ref),
                (bb_hbm, bb_ref),
                (uk_hbm, uk),
                (ub_hbm, ub_ref),
            )
            + tuple((bk_hbm.at[pl.ds(3 * n, 3)], bk.at[pl.ds(3 * n, 3)]) for n in range(9))
        )
    ]
    for load in loads:
        load.start()

    brick[0] = jnp.zeros_like(brick[0])
    brick[cx + 1] = jnp.zeros_like(brick[0])
    for y in (0, cy + 1):
        brick[1 : cx + 1, y] = jnp.zeros((cx, depth, pair), BF16)
    strip[0] = jnp.zeros_like(strip[0])
    strip[ngx * hx + 1] = jnp.zeros_like(strip[0])

    @pl.when(q == 0)
    def _():
        strip[1 : ngx * hx + 1, 0] = jnp.zeros((ngx * hx, depth, cd), BF16)

    @pl.when(q == nq - 1)
    def _():
        strip[1 : ngx * hx + 1, hy + 1] = jnp.zeros((ngx * hx, depth, cd), BF16)

    def valid(gg, qq):
        ok = jnp.logical_and(gg >= 0, gg < ngx)
        return jnp.logical_and(ok, jnp.logical_and(qq >= 0, qq < nq))

    barrier = pltpu.get_barrier_semaphore()

    def greet(gg, qq):
        pl.semaphore_signal(barrier, inc=1, device_id=device(gg, qq), device_id_type=MESH)

    partners = ngx - 1
    for b in (-1, 1):
        for a in (-1, 0, 1):
            there = valid(g + a, q + b)
            pl.when(there)(functools.partial(greet, g + a, q + b))
            partners += there.astype(jnp.int32)
    for d in range(1, ngx):
        greet(lax.rem(g + d, ngx), q)

    loads[0].wait()
    for x in range(cx):
        brick[1 + x, 1 : cy + 1] = (
            raw[x].astype(F32).reshape(cy, depth, pair).astype(BF16)
        )
    pl.semaphore_wait(barrier, partners)

    def remote(src, dst, send, recv, gg, qq):
        return pltpu.make_async_remote_copy(
            src_ref=src,
            dst_ref=dst,
            send_sem=send,
            recv_sem=recv,
            device_id=device(gg, qq),
            device_id_type=MESH,
        )

    def edges(step, count):
        if step == 0:
            return pl.ds(1, count), pl.ds(1, count)
        if step > 0:
            return pl.ds(count, 1), pl.ds(0, 1)
        return pl.ds(1, 1), pl.ds(count + 1, 1)

    halos = []
    for a in (-1, 0, 1):
        for b in (-1, 0, 1):
            if a == 0 and b == 0:
                continue
            t = len(halos)
            sx, dx = edges(a, cx)
            sy, dy = edges(b, cy)
            halos.append(
                (
                    valid(g + a, q + b),
                    remote(
                        brick.at[sx, sy], brick.at[dx, dy],
                        halo_send.at[t], halo_recv.at[t], g + a, q + b,
                    ),
                    valid(g - a, q - b),
                    remote(
                        brick.at[dx, dy], brick.at[dx, dy],
                        halo_send.at[t], halo_recv.at[t], g - a, q - b,
                    ),
                )
            )
    for ok, out, _, _ in halos:
        pl.when(ok)(out.start)

    loads[1].wait()
    empty = jnp.zeros((chans, chans), BF16)
    for ij in range(9):
        f0, f1, f2 = fk[3 * ij], fk[3 * ij + 1], fk[3 * ij + 2]
        band[ij * pair : ij * pair + chans] = jnp.concatenate([f1, f0, empty, f2], axis=1)
        band[ij * pair + chans : (ij + 1) * pair] = jnp.concatenate([f2, f1, f0, empty], axis=1)

    for _, _, ok, into in halos:
        pl.when(ok)(into.wait_recv)

    pieces = [
        brick[i : i + cx, j : j + cy].reshape(cx * cy * depth, pair)
        for i in range(3)
        for j in range(3)
    ]
    loads[2].wait()
    prod = jnp.dot(jnp.concatenate(pieces, axis=1), band[...], preferred_element_type=F32)
    side = prod[:, pair:]
    lane = lax.broadcasted_iota(jnp.int32, side.shape, 1)
    fb = fb_ref[...]
    total = (
        prod[:, :pair]
        + jnp.where(lane < chans, shifted(side, 1, depth), shifted(side, -1, depth))
        + jnp.concatenate([fb, fb], axis=1)
    )
    fine_ref[...] = silu(total).astype(BF16).reshape(cx, cy, depth, pair)

    loads[3].wait()
    loads[4].wait()
    cells = []
    for x in range(hx):
        for y in range(hy):
            cells.append(
                jnp.concatenate(
                    [fine_ref[2 * x + dx, 2 * y + dy] for dx in (0, 1) for dy in (0, 1)], axis=1
                )
            )
    coarse = jnp.dot(jnp.concatenate(cells, axis=0), dk[...], preferred_element_type=F32)
    coarse = silu(coarse + db_ref[...]).astype(BF16)
    strip[pl.ds(1 + hx * g, hx), 1 : hy + 1] = coarse.reshape(hx, hy, depth, cd)

    def planes(at):
        return pl.ds(1 + hx * at, hx)

    def block(source, to):
        ref = strip.at[planes(source), pl.ds(1, hy)]
        return remote(ref, ref, gather_send.at[to], gather_recv.at[source], to, q)

    def rim(at, b, sending):
        sy, dy = edges(b, hy)
        dst = strip.at[planes(at), dy]
        src = strip.at[planes(at), sy] if sending else dst
        t = (b + 1) // 2
        beside = q + b if sending else q - b
        return remote(src, dst, rim_send.at[at, t], rim_recv.at[at, t], g, beside)

    def rims(at, sending, action):
        for b in (-1, 1):
            other = q + b if sending else q - b
            pl.when(valid(g, other))(getattr(rim(at, b, sending), action))

    def others(visit):
        for d in range(1, ngx):
            for p in (g + d, g - d):
                pl.when(valid(p, q))(functools.partial(visit, p))

    others(lambda p: block(g, p).start())
    rims(g, True, "start")
    acc[...] = jnp.zeros_like(acc)
    for load in loads[5:]:
        load.wait()

    def part(source, columns):
        lhs = [strip[planes(source), j : j + hy].reshape(hx * hy * depth, cd) for j in columns]
        for i in range(3):
            at = pl.ds(2 + hx * source - i, hx)
            for k in range(3):
                term = sum(
                    jnp.dot(piece, bk[9 * i + 3 * j + k], preferred_element_type=F32)
                    for piece, j in zip(lhs, columns)
                )
                acc[k, at] += term.reshape(hx, hy * depth, cb)

    def source_of(n):
        return g + jnp.where(n % 2 == 1, (n + 1) // 2, -((n + 1) // 2))

    def swap(to, source):
        return remote(sent.at[to], back.at[source], swap_send.at[to], swap_recv.at[source], to, q)

    def finish(p):
        at = pl.ds(1 + hx * p, hx)
        taps = [acc[k, at].reshape(hx * hy * depth, cb) for k in range(3)]
        bottle = taps[1] + shifted(taps[0], 1, depth) + shifted(taps[2], -1, depth)
        return silu(bottle + bb_ref[...]).astype(BF16)

    def position(source):
        ahead = source - g
        return jnp.where(ahead > 0, 2 * ahead - 1, -2 * ahead)

    def last_step(p):
        far = position(p)
        for beside in (p - 1, p + 1):
            far = jnp.maximum(far, jnp.where(valid(beside, q), position(beside), 0))
        return far + 1

    @pl.loop(0, 2 * ngx)
    def _(n):
        now, before = source_of(n), source_of(n - 1)
        ready = jnp.logical_and(valid(now, q), n < 2 * ngx - 1)

        @pl.when(jnp.logical_and(ready, n > 0))
        def _():
            block(now, now).wait_recv()
            rims(now, True, "start")

        @pl.when(jnp.logical_and(valid(before, q), n > 0))
        def _():
            rims(before, False, "wait_recv")
            part(before, (0, 2))

        @pl.when(ready)
        def _():
            part(now, (1,))

        @pl.loop(0, ngx)
        def _(p):
            @pl.when(jnp.logical_and(p != g, last_step(p) == n))
            def _():
                sent[p] = finish(p)
                swap(p, g).start()

    lifted = jnp.dot(finish(g), uk[g], preferred_element_type=F32)
    for d in range(1, ngx):
        source = lax.rem(g + d, ngx)
        swap(source, source).wait_recv()
        lifted += jnp.dot(back[source], uk[source], preferred_element_type=F32)
    ub = ub_ref[...]
    ub = jnp.concatenate([ub, ub], axis=1)
    for x in range(hx):
        for dx in (0, 1):
            columns = []
            for y in range(hy):
                at = (x * hy + y) * depth
                for dy in (0, 1):
                    c = (2 * dx + dy) * pair
                    columns.append(
                        fine_ref[2 * x + dx, 2 * y + dy].astype(F32)
                        + (lifted[at : at + depth, c : c + pair] + ub)
                    )
            whole = jnp.stack(columns).reshape(cy, depth * pair)
            out_ref[2 * x + dx] = whole.astype(BF16)

    for ok, out, _, _ in halos:
        pl.when(ok)(out.wait_send)
    others(lambda p: block(g, p).wait_send())
    others(lambda p: swap(p, g).wait_send())
    for at in range(ngx):
        rims(at, True, "wait_send")


def local(
    sizes,
    volume,
    fine_kernel,
    fine_bias,
    down_kernel,
    down_bias,
    bottle_kernel,
    bottle_bias,
    up_kernel,
    up_bias,
):
    ngx = sizes[0]
    cx, cy, merged = volume.shape
    chans = fine_kernel.shape[1]
    pair = 2 * chans
    depth = merged // pair
    hx, hy = cx // 2, cy // 2
    cd = down_kernel.shape[1]
    cb = bottle_kernel.shape[2]
    cells = hx * hy * depth
    hbm = pl.BlockSpec(memory_space=pltpu.HBM)
    vmem = pl.BlockSpec(memory_space=pltpu.VMEM)
    dma = pltpu.SemaphoreType.DMA
    call = pl.pallas_call(
        functools.partial(body, sizes),
        out_shape=jax.ShapeDtypeStruct((cx, cy, merged), BF16),
        in_specs=[hbm] * 9,
        out_specs=vmem,
        scratch_shapes=[
            pltpu.VMEM(volume.shape, BF16),
            pltpu.VMEM((cx + 2, cy + 2, depth, pair), BF16),
            pltpu.VMEM(fine_kernel.shape, BF16),
            pltpu.VMEM((9 * pair, 2 * pair), BF16),
            pltpu.VMEM(down_kernel.shape, BF16),
            pltpu.VMEM(bottle_kernel.shape, BF16),
            pltpu.VMEM((ngx, cb, up_kernel.shape[1]), BF16),
            pltpu.VMEM((1, chans), F32),
            pltpu.VMEM((1, cd), F32),
            pltpu.VMEM((1, cb), F32),
            pltpu.VMEM((1, chans), F32),
            pltpu.VMEM((cx, cy, depth, pair), BF16),
            pltpu.VMEM((ngx * hx + 2, hy + 2, depth, cd), BF16),
            pltpu.VMEM((3, ngx * hx + 2, hy * depth, cb), F32),
            pltpu.VMEM((ngx, cells, cb), BF16),
            pltpu.VMEM((ngx, cells, cb), BF16),
            dma((17,)),
            dma((8,)),
            dma((8,)),
            dma((ngx,)),
            dma((ngx,)),
            dma((ngx, 2)),
            dma((ngx, 2)),
            dma((ngx,)),
            dma((ngx,)),
        ],
        compiler_params=pltpu.CompilerParams(
            collective_id=0, has_side_effects=True, vmem_limit_bytes=52 << 20
        ),
    )
    arrays = (
        volume,
        fine_kernel,
        fine_bias.reshape(1, -1),
        down_kernel,
        down_bias.reshape(1, -1),
        bottle_kernel,
        bottle_bias.reshape(1, -1),
        up_kernel.reshape(ngx, cb, -1),
        up_bias.reshape(1, -1),
    )
    return call(*(pltpu.with_memory_space_constraint(a, pltpu.HBM) for a in arrays))


def solution(mesh):
    placed = (
        P(("groups", "gx"), ("gy", "col"), None),
        P(),
        P(),
        P(),
        P(),
        P(None, None, "gx"),
        P("gx"),
        P(),
        P(),
    )
    sizes = tuple(mesh.shape[name] for name in ("gx", "gy", "col"))
    return jax.shard_map(
        functools.partial(local, sizes),
        mesh=mesh,
        in_specs=placed,
        out_specs=P(("groups", "gx"), ("gy", "col"), None),
        check_vma=False,
    )
```

```python
import functools

import jax
import jax.numpy as jnp
from jax import lax
from jax.experimental import pallas as pl
from jax.experimental.pallas import tpu as pltpu
from jax.sharding import PartitionSpec as P

MESH = pl.DeviceIdType.MESH
F32 = jnp.float32
BF16 = jnp.bfloat16


def silu(a):
    return (0.5 * a) * (1.0 + jnp.tanh(0.5 * a))


def shifted(a, amount, depth):
    rows = a.shape[0]
    z = lax.broadcasted_iota(jnp.int32, a.shape, 0) % depth
    moved = pltpu.roll(a, amount % rows, 0)
    keep = z >= amount if amount > 0 else z < depth + amount
    return jnp.where(keep, moved, 0.0)


def body(
    sizes,
    vol_hbm,
    fk_hbm,
    fb_hbm,
    dk_hbm,
    db_hbm,
    bk_hbm,
    bb_hbm,
    uk_hbm,
    ub_hbm,
    out_ref,
    raw,
    brick,
    fk,
    band,
    dk,
    bk,
    uk,
    fb_ref,
    db_ref,
    bb_ref,
    ub_ref,
    fine_ref,
    strip,
    acc,
    sent,
    back,
    load_sem,
    halo_send,
    halo_recv,
    gather_send,
    gather_recv,
    rim_send,
    rim_recv,
    swap_send,
    swap_recv,
):
    ngx, ngy, ncol = sizes
    nq = ngy * ncol
    cx, cy, depth, pair = fine_ref.shape
    chans = pair // 2
    hx, hy = cx // 2, cy // 2
    cd = dk.shape[1]
    cb = bk.shape[2]
    g = lax.axis_index("gx")
    q = lax.axis_index("gy") * ncol + lax.axis_index("col")

    def device(gg, qq):
        return {"gx": gg, "gy": qq // ncol, "col": qq % ncol}

    loads = [
        pltpu.make_async_copy(src, dst, load_sem.at[n])
        for n, (src, dst) in enumerate(
            (
                (vol_hbm, raw),
                (fk_hbm, fk),
                (fb_hbm, fb_ref),
                (dk_hbm, dk),
                (db_hbm, db_ref),
                (bb_hbm, bb_ref),
                (uk_hbm, uk),
                (ub_hbm, ub_ref),
            )
            + tuple((bk_hbm.at[pl.ds(3 * n, 3)], bk.at[pl.ds(3 * n, 3)]) for n in range(9))
        )
    ]
    for load in loads:
        load.start()

    brick[0] = jnp.zeros_like(brick[0])
    brick[cx + 1] = jnp.zeros_like(brick[0])
    for y in (0, cy + 1):
        brick[1 : cx + 1, y] = jnp.zeros((cx, depth, pair), BF16)
    strip[0] = jnp.zeros_like(strip[0])
    strip[ngx * hx + 1] = jnp.zeros_like(strip[0])

    @pl.when(q == 0)
    def _():
        strip[1 : ngx * hx + 1, 0] = jnp.zeros((ngx * hx, depth, cd), BF16)

    @pl.when(q == nq - 1)
    def _():
        strip[1 : ngx * hx + 1, hy + 1] = jnp.zeros((ngx * hx, depth, cd), BF16)

    def valid(gg, qq):
        ok = jnp.logical_and(gg >= 0, gg < ngx)
        return jnp.logical_and(ok, jnp.logical_and(qq >= 0, qq < nq))

    barrier = pltpu.get_barrier_semaphore()

    def greet(gg, qq):
        pl.semaphore_signal(barrier, inc=1, device_id=device(gg, qq), device_id_type=MESH)

    partners = ngx - 1
    for b in (-1, 1):
        for a in (-1, 0, 1):
            there = valid(g + a, q + b)
            pl.when(there)(functools.partial(greet, g + a, q + b))
            partners += there.astype(jnp.int32)
    for d in range(1, ngx):
        greet(lax.rem(g + d, ngx), q)

    loads[0].wait()
    for x in range(cx):
        brick[1 + x, 1 : cy + 1] = (
            raw[x].astype(F32).reshape(cy, depth, pair).astype(BF16)
        )
    pl.semaphore_wait(barrier, partners)

    def remote(src, dst, send, recv, gg, qq):
        return pltpu.make_async_remote_copy(
            src_ref=src,
            dst_ref=dst,
            send_sem=send,
            recv_sem=recv,
            device_id=device(gg, qq),
            device_id_type=MESH,
        )

    def edges(step, count):
        if step == 0:
            return pl.ds(1, count), pl.ds(1, count)
        if step > 0:
            return pl.ds(count, 1), pl.ds(0, 1)
        return pl.ds(1, 1), pl.ds(count + 1, 1)

    halos = []
    for a in (-1, 0, 1):
        for b in (-1, 0, 1):
            if a == 0 and b == 0:
                continue
            t = len(halos)
            sx, dx = edges(a, cx)
            sy, dy = edges(b, cy)
            halos.append(
                (
                    valid(g + a, q + b),
                    remote(
                        brick.at[sx, sy], brick.at[dx, dy],
                        halo_send.at[t], halo_recv.at[t], g + a, q + b,
                    ),
                    valid(g - a, q - b),
                    remote(
                        brick.at[dx, dy], brick.at[dx, dy],
                        halo_send.at[t], halo_recv.at[t], g - a, q - b,
                    ),
                )
            )
    for ok, out, _, _ in halos:
        pl.when(ok)(out.start)

    loads[1].wait()
    empty = jnp.zeros((chans, chans), BF16)
    for ij in range(9):
        f0, f1, f2 = fk[3 * ij], fk[3 * ij + 1], fk[3 * ij + 2]
        band[ij * pair : ij * pair + chans] = jnp.concatenate([f1, f0, empty, f2], axis=1)
        band[ij * pair + chans : (ij + 1) * pair] = jnp.concatenate([f2, f1, f0, empty], axis=1)

    for _, _, ok, into in halos:
        pl.when(ok)(into.wait_recv)

    pieces = [
        brick[i : i + cx, j : j + cy].reshape(cx * cy * depth, pair)
        for i in range(3)
        for j in range(3)
    ]
    loads[2].wait()
    prod = jnp.dot(jnp.concatenate(pieces, axis=1), band[...], preferred_element_type=F32)
    side = prod[:, pair:]
    lane = lax.broadcasted_iota(jnp.int32, side.shape, 1)
    fb = fb_ref[...]
    total = (
        prod[:, :pair]
        + jnp.where(lane < chans, shifted(side, 1, depth), shifted(side, -1, depth))
        + jnp.concatenate([fb, fb], axis=1)
    )
    fine_ref[...] = silu(total).astype(BF16).reshape(cx, cy, depth, pair)

    loads[3].wait()
    loads[4].wait()
    cells = []
    for x in range(hx):
        for y in range(hy):
            cells.append(
                jnp.concatenate(
                    [fine_ref[2 * x + dx, 2 * y + dy] for dx in (0, 1) for dy in (0, 1)], axis=1
                )
            )
    coarse = jnp.dot(jnp.concatenate(cells, axis=0), dk[...], preferred_element_type=F32)
    coarse = silu(coarse + db_ref[...]).astype(BF16)
    strip[pl.ds(1 + hx * g, hx), 1 : hy + 1] = coarse.reshape(hx, hy, depth, cd)

    def planes(at):
        return pl.ds(1 + hx * at, hx)

    def block(source, to):
        ref = strip.at[planes(source), pl.ds(1, hy)]
        return remote(ref, ref, gather_send.at[to], gather_recv.at[source], to, q)

    def rim(at, b, sending):
        sy, dy = edges(b, hy)
        dst = strip.at[planes(at), dy]
        src = strip.at[planes(at), sy] if sending else dst
        t = (b + 1) // 2
        beside = q + b if sending else q - b
        return remote(src, dst, rim_send.at[at, t], rim_recv.at[at, t], g, beside)

    def rims(at, sending, action):
        for b in (-1, 1):
            other = q + b if sending else q - b
            pl.when(valid(g, other))(getattr(rim(at, b, sending), action))

    def others(visit):
        for d in range(ngx - 1, 0, -1):
            for p in (g + d, g - d):
                pl.when(valid(p, q))(functools.partial(visit, p))

    rims(g, True, "start")
    others(lambda p: block(g, p).start())
    acc[...] = jnp.zeros_like(acc)
    for load in loads[5:]:
        load.wait()

    def part(source, columns):
        lhs = [strip[planes(source), j : j + hy].reshape(hx * hy * depth, cd) for j in columns]
        for i in range(3):
            at = pl.ds(2 + hx * source - i, hx)
            for k in range(3):
                term = sum(
                    jnp.dot(piece, bk[9 * i + 3 * j + k], preferred_element_type=F32)
                    for piece, j in zip(lhs, columns)
                )
                acc[k, at] += term.reshape(hx, hy * depth, cb)

    def source_of(n):
        return g + jnp.where(n % 2 == 1, (n + 1) // 2, -((n + 1) // 2))

    def swap(to, source):
        return remote(sent.at[to], back.at[source], swap_send.at[to], swap_recv.at[source], to, q)

    def finish(p):
        at = pl.ds(1 + hx * p, hx)
        taps = [acc[k, at].reshape(hx * hy * depth, cb) for k in range(3)]
        bottle = taps[1] + shifted(taps[0], 1, depth) + shifted(taps[2], -1, depth)
        return silu(bottle + bb_ref[...]).astype(BF16)

    def position(source):
        ahead = source - g
        return jnp.where(ahead > 0, 2 * ahead - 1, -2 * ahead)

    def last_step(p):
        far = position(p)
        for beside in (p - 1, p + 1):
            far = jnp.maximum(far, jnp.where(valid(beside, q), position(beside), 0))
        return far + 1

    @pl.loop(0, 2 * ngx)
    def _(n):
        now, before = source_of(n), source_of(n - 1)
        ready = jnp.logical_and(valid(now, q), n < 2 * ngx - 1)

        @pl.when(jnp.logical_and(ready, n > 0))
        def _():
            block(now, now).wait_recv()
            rims(now, True, "start")

        @pl.when(jnp.logical_and(valid(before, q), n > 0))
        def _():
            rims(before, False, "wait_recv")
            part(before, (0, 2))

        @pl.when(ready)
        def _():
            part(now, (1,))

        @pl.loop(0, ngx)
        def _(p):
            @pl.when(jnp.logical_and(p != g, last_step(p) == n))
            def _():
                sent[p] = finish(p)
                swap(p, g).start()

    lifted = jnp.dot(finish(g), uk[g], preferred_element_type=F32)
    for d in range(1, ngx):
        source = lax.rem(g + d, ngx)
        swap(source, source).wait_recv()
        lifted += jnp.dot(back[source], uk[source], preferred_element_type=F32)
    ub = ub_ref[...]
    ub = jnp.concatenate([ub, ub], axis=1)
    for x in range(hx):
        for dx in (0, 1):
            columns = []
            for y in range(hy):
                at = (x * hy + y) * depth
                for dy in (0, 1):
                    c = (2 * dx + dy) * pair
                    columns.append(
                        fine_ref[2 * x + dx, 2 * y + dy].astype(F32)
                        + (lifted[at : at + depth, c : c + pair] + ub)
                    )
            whole = jnp.stack(columns).reshape(cy, depth * pair)
            out_ref[2 * x + dx] = whole.astype(BF16)

    for ok, out, _, _ in halos:
        pl.when(ok)(out.wait_send)
    others(lambda p: block(g, p).wait_send())
    others(lambda p: swap(p, g).wait_send())
    for at in range(ngx):
        rims(at, True, "wait_send")


def local(
    sizes,
    volume,
    fine_kernel,
    fine_bias,
    down_kernel,
    down_bias,
    bottle_kernel,
    bottle_bias,
    up_kernel,
    up_bias,
):
    ngx = sizes[0]
    cx, cy, merged = volume.shape
    chans = fine_kernel.shape[1]
    pair = 2 * chans
    depth = merged // pair
    hx, hy = cx // 2, cy // 2
    cd = down_kernel.shape[1]
    cb = bottle_kernel.shape[2]
    cells = hx * hy * depth
    hbm = pl.BlockSpec(memory_space=pltpu.HBM)
    vmem = pl.BlockSpec(memory_space=pltpu.VMEM)
    dma = pltpu.SemaphoreType.DMA
    call = pl.pallas_call(
        functools.partial(body, sizes),
        out_shape=jax.ShapeDtypeStruct((cx, cy, merged), BF16),
        in_specs=[hbm] * 9,
        out_specs=vmem,
        scratch_shapes=[
            pltpu.VMEM(volume.shape, BF16),
            pltpu.VMEM((cx + 2, cy + 2, depth, pair), BF16),
            pltpu.VMEM(fine_kernel.shape, BF16),
            pltpu.VMEM((9 * pair, 2 * pair), BF16),
            pltpu.VMEM(down_kernel.shape, BF16),
            pltpu.VMEM(bottle_kernel.shape, BF16),
            pltpu.VMEM((ngx, cb, up_kernel.shape[1]), BF16),
            pltpu.VMEM((1, chans), F32),
            pltpu.VMEM((1, cd), F32),
            pltpu.VMEM((1, cb), F32),
            pltpu.VMEM((1, chans), F32),
            pltpu.VMEM((cx, cy, depth, pair), BF16),
            pltpu.VMEM((ngx * hx + 2, hy + 2, depth, cd), BF16),
            pltpu.VMEM((3, ngx * hx + 2, hy * depth, cb), F32),
            pltpu.VMEM((ngx, cells, cb), BF16),
            pltpu.VMEM((ngx, cells, cb), BF16),
            dma((17,)),
            dma((8,)),
            dma((8,)),
            dma((ngx,)),
            dma((ngx,)),
            dma((ngx, 2)),
            dma((ngx, 2)),
            dma((ngx,)),
            dma((ngx,)),
        ],
        compiler_params=pltpu.CompilerParams(
            collective_id=0, has_side_effects=True, vmem_limit_bytes=52 << 20
        ),
    )
    arrays = (
        volume,
        fine_kernel,
        fine_bias.reshape(1, -1),
        down_kernel,
        down_bias.reshape(1, -1),
        bottle_kernel,
        bottle_bias.reshape(1, -1),
        up_kernel.reshape(ngx, cb, -1),
        up_bias.reshape(1, -1),
    )
    return call(*(pltpu.with_memory_space_constraint(a, pltpu.HBM) for a in arrays))


def solution(mesh):
    placed = (
        P(("groups", "gx"), ("gy", "col"), None),
        P(),
        P(),
        P(),
        P(),
        P(None, None, "gx"),
        P("gx"),
        P(),
        P(),
    )
    sizes = tuple(mesh.shape[name] for name in ("gx", "gy", "col"))
    return jax.shard_map(
        functools.partial(local, sizes),
        mesh=mesh,
        in_specs=placed,
        out_specs=P(("groups", "gx"), ("gy", "col"), None),
        check_vma=False,
    )
```
